32 devices in a mesh: hop: 4 (over z), node: 8 (over y, x, core).
Axes of the slice: x: 2, y: 2, z: 4, core: 2. Of those that a mesh axis runs over, the one named last changes fastest.
Arguments:
- child_features: bfloat16 [16384, 1024], P(('hop', 'node')), may hold values from -6 to 6
- child_type: int32 [16384], P(('hop', 'node')), may hold values 0 or 1
- parent_features: bfloat16 [16384, 1024], P(('hop', 'node')), may hold values from -6 to 6
- child_slot: int32 [32, 32, 32], P(('hop', 'node')), may hold values from 0 to 511
- parent_slot: int32 [32, 32, 32], P(('hop', 'node')), may hold values from 0 to 511
- importance: int32 [32, 32, 32], P(('hop', 'node')), may hold values from 0 to 16, as said below
- board_proj: bfloat16 [512, 1024], replicated, may hold values from -0.25 to 0.25
- board_bias: float32 [1024], replicated, may hold values from -3 to 3
- neigh_weight: bfloat16 [1024, 1024], replicated, may hold values from -0.1875 to 0.1875
- neigh_bias: float32 [1024], replicated, may hold values from -3 to 3
- comb_weight: bfloat16 [2048, 1024], replicated, may hold values from -0.125 to 0.125
- comb_bias: float32 [1024], replicated, may hold values from -3 to 3
- out_grad: bfloat16 [16384, 1024], P(('hop', 'node')), may hold values from -6 to 6
Outputs:
- embedding: bfloat16 [16384, 1024], P(('hop', 'node'))
- child_grad: bfloat16 [16384, 1024], P(('hop', 'node'))
- parent_grad: bfloat16 [16384, 1024], P(('hop', 'node'))
- board_proj_grad: float32 [512, 1024], replicated
- board_bias_grad: float32 [1024], replicated
- neigh_weight_grad: float32 [1024, 1024], replicated
- neigh_bias_grad: float32 [1024], replicated
- comb_weight_grad: float32 [2048, 1024], replicated
- comb_bias_grad: float32 [1024], replicated
The draws below stay inside these ranges and needn't reach their ends.
Inputs may be any that keep to these rules, and one draw needn't show every extreme that they name: For receiver r and sender s, importance[r, s, k] is positive for k below a count c(r, s) and 0 from there on; c(r, s) <= 32, and in every draw one receiver has c = 32 from every sender.
All inputs are finite; a program needn't handle non-finite values. No bound on the sum of `child_type` on one device may be relied on, other than what follows from the above.
Results may differ from the reference program's by a relative error of at most 0.0069.
Values may be sent and summed in bfloat16 or wider, within the bound.
A program may use at most 128 MiB of HBM per device.

```python
import jax
import jax.numpy as jnp
from jax import lax

FEAT = 1024
BOARD = 512
HIDDEN_SIZE = 1024
OUT = 1024
CH_DEV = 512
PAR_DEV = 512
SENDERS = 32
CAP = 32
CHILDREN = 16384
PARENTS = 16384


def draw_importance(key, part):
    key_busy, key_count, key_value = jax.random.split(jax.random.fold_in(key, 17), 3)
    busiest = jax.random.randint(key_busy, (), 0, SENDERS)
    counts = jax.random.randint(key_count, (SENDERS, SENDERS), CAP // 4, 3 * CAP // 4 + 1)
    receiver = jnp.arange(SENDERS, dtype=jnp.int32)[:, None]
    counts = jnp.where(receiver == busiest, CAP, counts)
    values = jax.random.randint(key_value, (SENDERS, SENDERS, CAP), 1, 17)
    live = jnp.arange(CAP, dtype=jnp.int32)[None, None, :] < counts[:, :, None]
    return jnp.where(live, values, 0).astype(jnp.int32)


def set_ends(entries, rng, least, largest):
    longest = entries.shape.index(max(entries.shape))
    spots = []
    for shift in (0, 1):
        where = [jax.random.randint(jax.random.fold_in(rng, axis), (), 0, length) for axis, length in enumerate(entries.shape)]
        where[longest] = (where[longest] + shift) % entries.shape[longest]
        spots.append(tuple(where))
    return entries.at[spots[0]].set(least).at[spots[1]].set(largest)


def block_scale(key, extent, pieces, least, high):
    def one(axis_at, blocks):
        steps = jax.random.uniform(jax.random.fold_in(jax.random.fold_in(key, 6), axis_at), (blocks,), jnp.float32, least / len(pieces), high / len(pieces))
        return jnp.repeat(jnp.exp(steps), extent[axis_at] // blocks).reshape((-1,) + (1,) * (len(extent) - axis_at - 1))

    factor_of = one(*pieces[0])
    for cut in pieces[1:]:
        factor_of = factor_of * one(*cut)
    return factor_of


def noise(key, shape, width, most, cuts=(), kind=jnp.bfloat16):
    result = width * jax.random.normal(key, shape, jnp.float32)
    if cuts:
        result = result * block_scale(key, shape, cuts, -0.22, 0.18)
    return jnp.clip(result, -most, most).astype(kind)


def setup_inputs(seed: int = 0) -> dict:
    arg_keys = jax.random.split(jax.random.key(seed), 14)
    child_features = noise(arg_keys[0], (CHILDREN, FEAT), 1.0, 6.0, ((0, 32),))
    child_type = set_ends((jax.random.randint(arg_keys[1], (CHILDREN,), 0, 3) < 1).astype(jnp.int32), jax.random.fold_in(arg_keys[1], 1), 0, 1)
    parent_features = noise(arg_keys[2], (PARENTS, FEAT), 1.0, 6.0, ((0, 32),))
    child_slot = set_ends(jax.random.randint(arg_keys[3], (SENDERS, SENDERS, CAP), 0, CH_DEV), jax.random.fold_in(arg_keys[3], 1), 0, CH_DEV - 1).astype(jnp.int32)
    parent_slot = set_ends(jax.random.randint(arg_keys[4], (SENDERS, SENDERS, CAP), 0, PAR_DEV), jax.random.fold_in(arg_keys[4], 1), 0, PAR_DEV - 1).astype(jnp.int32)
    importance = draw_importance(jax.random.fold_in(arg_keys[13], 71), 0)
    board_proj = noise(arg_keys[6], (BOARD, FEAT), BOARD ** -0.5, 0.25)
    board_bias = noise(arg_keys[7], (FEAT,), 0.5, 3.0, (), jnp.float32)
    neigh_weight = noise(arg_keys[8], (FEAT, HIDDEN_SIZE), FEAT ** -0.5, 0.1875)
    neigh_bias = noise(arg_keys[9], (HIDDEN_SIZE,), 0.5, 3.0, (), jnp.float32)
    comb_weight = noise(arg_keys[10], (FEAT + HIDDEN_SIZE, OUT), (FEAT + HIDDEN_SIZE) ** -0.5, 0.125)
    comb_bias = noise(arg_keys[11], (OUT,), 0.5, 3.0, (), jnp.float32)
    out_grad = noise(arg_keys[12], (PARENTS, OUT), 1.0, 6.0, ((0, 32),))
    return dict(child_features=child_features, child_type=child_type, parent_features=parent_features, child_slot=child_slot, parent_slot=parent_slot, importance=importance, board_proj=board_proj, board_bias=board_bias, neigh_weight=neigh_weight, neigh_bias=neigh_bias, comb_weight=comb_weight, comb_bias=comb_bias, out_grad=out_grad)


@jax.custom_vjp
def low(v):
    return lax.optimization_barrier(v.astype(jnp.bfloat16)).astype(jnp.float32)

@jax.custom_vjp
def low_back(v):
    return v

def low_keep(v):
    return (low(v), None)

def low_pass(kept, grad):
    return (grad,)

def back_keep(v):
    return (v, None)

def back_low(kept, grad):
    return (low(grad),)
low.defvjp(low_keep, low_pass)
low_back.defvjp(back_keep, back_low)
epsilon = 1e-06

def reference(child_features, child_type, parent_features, child_slot, parent_slot, importance, board_proj, board_bias, neigh_weight, neigh_bias, comb_weight, comb_bias, out_grad):
    highest = lax.Precision.HIGHEST
    board = (child_type == 1)[:, None]
    sender_base = jnp.arange(SENDERS, dtype=jnp.int32)[:, None, None] * CH_DEV
    child_global = (sender_base + child_slot).astype(jnp.int32)
    by_receiver = jnp.transpose(child_global, (1, 0, 2)).reshape(SENDERS, SENDERS * CAP)
    weights = importance.astype(jnp.float32).reshape(SENDERS, SENDERS * CAP)
    targets = parent_slot.reshape(SENDERS, SENDERS * CAP).astype(jnp.int32)

    def forward(features, parents, proj, proj_bias, neigh_w, neigh_b, comb_w, comb_b):
        board_pre = low_back(jnp.dot(features[:, :BOARD], proj, precision=highest) + proj_bias)
        child_in = jnp.where(board, board_pre, features)
        neigh_pre = low_back(jnp.dot(low(child_in), neigh_w, precision=highest) + neigh_b)
        neigh = low(jax.nn.silu(neigh_pre))

        def receive(item):
            rows, wts, tgt = item
            message = low_back(neigh[rows])
            sums = jax.ops.segment_sum(message * wts[:, None], tgt, num_segments=PAR_DEV)
            total = jax.ops.segment_sum(wts, tgt, num_segments=PAR_DEV)
            return sums / jnp.maximum(total, 1.0)[:, None]
        agg = lax.map(jax.checkpoint(receive), (by_receiver, weights, targets)).reshape(PARENTS, HIDDEN_SIZE)
        cat = jnp.concatenate([parents, low(agg)], axis=1)
        comb_pre = low_back(jnp.dot(cat, comb_w, precision=highest) + comb_b)
        hidden_z = jax.nn.silu(comb_pre)
        return hidden_z * lax.rsqrt(lax.optimization_barrier(jnp.sum(hidden_z * hidden_z, axis=1, keepdims=True)) + epsilon)
    primals = (child_features.astype(jnp.float32), parent_features.astype(jnp.float32), board_proj.astype(jnp.float32), board_bias, neigh_weight.astype(jnp.float32), neigh_bias, comb_weight.astype(jnp.float32), comb_bias)
    embedded, pull = jax.vjp(forward, *primals)
    grads = pull(out_grad.astype(jnp.float32))
    return (embedded.astype(jnp.bfloat16), grads[0].astype(jnp.bfloat16), grads[1].astype(jnp.bfloat16), grads[2], grads[3], grads[4], grads[5], grads[6], grads[7])
```

```python
import functools

import jax
import jax.numpy as jnp
from jax import lax
from jax.experimental import pallas as pl
from jax.experimental.pallas import tpu as pltpu
from jax.sharding import PartitionSpec as P

epsilon = 1e-06
MESH = pl.DeviceIdType.MESH
AXES = ("hop", "node")
f32, bf16 = jnp.float32, jnp.bfloat16


def dot(a, b):
    return jnp.dot(a, b, preferred_element_type=f32)


def outer_sum(left, right):
    return lax.dot_general(left, right, (((0,), (0,)), ((), ())), preferred_element_type=f32)


def times_transposed(left, right):
    return lax.dot_general(left, right, (((1,), (1,)), ((), ())), preferred_element_type=f32)


def silu_slope(value):
    sigma = jax.nn.sigmoid(value)
    return sigma * (1.0 + value * (1.0 - sigma))


def each(count, size, step):
    def one(index, carry):
        step(pl.multiple_of(index * size, size))
        return carry

    lax.fori_loop(0, count // size, one, 0)


class Net:
    def __init__(self, n, node):
        self.n, self.node = n, node
        self.me = lax.axis_index("hop") * node + lax.axis_index("node")
        self.bits = [1 << b for b in range(n.bit_length() - 1)]
        self.bit = {b: (self.me // b) % 2 for b in self.bits}

    def partner(self, mask):
        index = 0
        for b in self.bits:
            index = index + ((self.bit[b] + (mask // b) % 2) % 2) * b
        return (index // self.node, index % self.node), index


class Sems:
    def __init__(self, send, recv):
        self.send, self.recv, self.used = send, recv, 0

    def copy(self, src, dst, where):
        at = self.used
        self.used += 1
        made = pltpu.make_async_remote_copy(
            src_ref=src, dst_ref=dst, send_sem=self.send.at[at], recv_sem=self.recv.at[at],
            device_id=where, device_id_type=MESH,
        )
        made.start()
        return made


def reduce_stream(net, sems, grad, landing, full, first, rows, stages):
    off, length, land = first, rows, first
    trail = []
    for at_stage, bits in enumerate(stages):
        ways = 1 << len(bits)
        part = length // ways
        result = full if at_stage == len(stages) - 1 else grad
        mine = sum(net.bit[b] * (1 << i) for i, b in enumerate(bits))
        sent = []
        for c in range(1, ways):
            mask = sum(b for i, b in enumerate(bits) if (c >> i) & 1)
            theirs = sum(((net.bit[b] + ((c >> i) & 1)) % 2) * (1 << i) for i, b in enumerate(bits))
            src = grad.at[pl.ds(pl.multiple_of(off + theirs * part, 16), part)]
            dst = landing.at[pl.ds(land + (c - 1) * part, part)]
            sent.append(sems.copy(src, dst, net.partner(mask)[0]))
        yield
        for made in sent:
            made.wait()
        keep = off + mine * part
        block = min(part, 64)

        def add(r):
            at = pl.ds(pl.multiple_of(keep + r, 16), block)
            total = grad[at, :].astype(f32)
            for c in range(1, ways):
                total = total + landing[pl.ds(pl.multiple_of(land + (c - 1) * part + r, 16), block), :].astype(f32)
            result[at, :] = total.astype(bf16)

        each(part, block, add)
        trail.append((bits, off, length))
        off, length, land = keep, part, land + (ways - 1) * part
    for bits, whole, size in reversed(trail):
        at = pl.ds(pl.multiple_of(off, 16), length)
        sent = []
        for c in range(1, 1 << len(bits)):
            mask = sum(b for i, b in enumerate(bits) if (c >> i) & 1)
            sent.append(sems.copy(full.at[at], full.at[at], net.partner(mask)[0]))
        yield
        for made in sent:
            made.wait()
        off, length = whole, size


def bias_stream(net, sems, total, landing):
    for i, b in enumerate(net.bits):
        made = sems.copy(total, landing.at[i], net.partner(b)[0])
        yield
        made.wait()
        total[...] = total[...] + landing[i]


def kernel(
    n, node,
    ct, cs, ps, im, bb, nb, cb, cf_h, pf_h, bp_h, nw_h, cw_h, og_h,
    emb_h, cgr_h, pgr_h, gc_h, gn_h, gb_h, bias_h,
    cf, pf, bp, nw, cw, og,
    mask, ci, slope, ng, pick, pick_t, spread, spread_t, inv,
    out_f, in_f, out_b, in_b,
    comb, agg, agg_t, pf_t, ci_t, cf_t, gcomb, gnp, emb,
    gc, rc, gc_sum, gt, rt, gt_sum, bias_c, bias_t, land_c, land_t,
    in_sem, out_sem, a_send, a_recv, r_send, r_recv,
):
    pgr, cgr, gbd = ng, pf, og
    net = Net(n, node)
    sems = Sems(r_send, r_recv)
    me = net.me
    senders, cap = cs.shape
    edges = senders * cap
    children, feat = cf.shape
    parents = pf.shape[0]
    board = bp.shape[0]
    hidden = nw.shape[1]
    half = hidden // 2

    barrier = pltpu.get_barrier_semaphore()

    def greet(i, carry):
        pl.semaphore_signal(barrier, inc=1, device_id=net.partner(i)[0], device_id_type=MESH)
        return carry

    lax.fori_loop(1, n, greet, 0)

    loads = {}
    for i, (name, src, dst) in enumerate(
        [("cf", cf_h, cf), ("bp", bp_h, bp), ("nw", nw_h, nw), ("pf", pf_h, pf), ("cw", cw_h, cw), ("og", og_h, og)]
    ):
        loads[name] = pltpu.make_async_copy(src, dst, in_sem.at[i])
        loads[name].start()

    wide = 128
    eye = lax.broadcasted_iota(jnp.int32, (wide, wide), 0) == lax.broadcasted_iota(jnp.int32, (wide, wide), 1)
    for q in range(ct.shape[0]):
        row = ct[q : q + 1, :].astype(f32)
        mask[pl.ds(q * wide, wide), :] = jnp.sum(jnp.where(eye, row, 0.0), axis=1, keepdims=True)
    small = lax.broadcasted_iota(jnp.int32, (cap, cap), 0) == lax.broadcasted_iota(jnp.int32, (cap, cap), 1)

    def column(ref, s):
        return jnp.sum(jnp.where(small, ref[pl.ds(s, 1), :].astype(f32), 0.0), axis=1, keepdims=True)

    child_lane = lax.broadcasted_iota(jnp.int32, (cap, children), 1).astype(f32)
    parent_lane = lax.broadcasted_iota(jnp.int32, (cap, parents), 1).astype(f32)

    def make_pick(s, carry):
        hit = column(cs, s) == child_lane
        pick[pl.ds(pl.multiple_of(s * cap, 16), cap), :] = jnp.where(hit, 1.0, 0.0).astype(bf16)
        return carry

    lax.fori_loop(0, senders, make_pick, 0)

    loads["cf"].wait()
    loads["bp"].wait()

    def project(c):
        at = pl.ds(c, 256)
        pre = dot(cf[:, 0:board], bp[:, at]) + bb[:, at]
        ci[:, at] = jnp.where(mask[...] > 0.5, pre.astype(bf16), cf[:, at])

    each(feat, 256, project)
    loads["nw"].wait()

    def transform(c):
        at = pl.ds(c, 256)
        pre = dot(ci[...], nw[:, at]) + nb[:, at]
        slope[:, at] = pre
        ng[:, at] = (pre * jax.nn.sigmoid(pre)).astype(bf16)

    each(hidden, 256, transform)

    a_order = n // 2

    def send_all(out, into, h, which):
        def one(i, carry):
            far = i % 2 == 0
            m = jnp.where(far, n - 1 - i // 2, (i + 1) // 2)
            where, index = net.partner(m)
            pltpu.make_async_remote_copy(
                src_ref=out.at[h, pl.ds(pl.multiple_of(index * cap, 16), cap)],
                dst_ref=into.at[h, pl.ds(pl.multiple_of(me * cap, 16), cap)],
                send_sem=a_send.at[which], recv_sem=a_recv.at[which],
                device_id=where, device_id_type=MESH,
            ).start()
            return carry

        lax.fori_loop(0, n - 1, one, 0)
        own = pl.ds(pl.multiple_of(me * cap, 16), cap)
        into[h, own, :] = out[h, own, :]

    def all_of(out, into, h, which):
        return pltpu.make_async_remote_copy(
            src_ref=out.at[h, pl.ds(0, edges - cap)], dst_ref=into.at[h, pl.ds(0, edges - cap)],
            send_sem=a_send.at[which], recv_sem=a_recv.at[which],
            device_id=net.partner(1)[0], device_id_type=MESH,
        )

    for h in range(2):
        def gather(c):
            out_f[h, :, pl.ds(c, 256)] = dot(pick[...], ng[:, pl.ds(pl.multiple_of(h * half + c, 256), 256)]).astype(bf16)

        each(half, 256, gather)
        if h == 0:
            pl.semaphore_wait(barrier, n - 1)
        send_all(out_f, in_f, h, h)

    def make_spread(s, carry):
        hit = column(ps, s) == parent_lane
        spread[pl.ds(pl.multiple_of(s * cap, 16), cap), :] = jnp.where(hit, column(im, s), 0.0).astype(bf16)
        return carry

    lax.fori_loop(0, senders, make_spread, 0)
    spread_t[...] = spread[...].T
    totals = dot(spread_t[...], jnp.ones((edges, 128), bf16))
    inv[...] = 1.0 / jnp.maximum(totals[:, 0:1], 1.0)
    loads["pf"].wait()
    loads["cw"].wait()
    loads["og"].wait()

    def parent_part(c):
        at = pl.ds(c, 256)
        comb[:, at] = dot(pf[...], cw[0:feat, at]) + cb[:, at]

    each(feat, 256, parent_part)
    pick_t[...] = pick[...].T
    pf_t[...] = pf[...].T
    ci_t[...] = ci[...].T
    cf_t[...] = cf[:, 0:board].T

    def to_slope(r):
        at = pl.ds(r, 32)
        slope[at, :] = silu_slope(slope[at, :])

    each(children, 32, to_slope)

    for h in range(2):
        all_of(out_f, in_f, h, h).wait_recv()

        def aggregate(c):
            sums = dot(spread_t[...], in_f[h, :, pl.ds(c, 256)]) * inv[...]
            agg[:, pl.ds(pl.multiple_of(h * half + c, 256), 256)] = sums.astype(bf16)

        each(half, 256, aggregate)

        def combine(c):
            at = pl.ds(c, 256)
            comb[:, at] += dot(agg[:, h * half : (h + 1) * half], cw[feat + h * half : feat + (h + 1) * half, at])

        each(feat, 256, combine)

    bias_c[...] = jnp.zeros_like(bias_c)

    def normalize(r):
        at = pl.ds(r, 32)
        pre = comb[at, :]
        sigma = jax.nn.sigmoid(pre)
        z = pre * sigma
        inverse = lax.rsqrt(jnp.sum(z * z, axis=1, keepdims=True) + epsilon)
        y = z * inverse
        emb[at, :] = y.astype(bf16)
        gy = og[at, :].astype(f32)
        gz = inverse * (gy - y * jnp.sum(y * gy, axis=1, keepdims=True))
        g = (gz * (sigma * (1.0 + pre * (1.0 - sigma)))).astype(bf16)
        gcomb[at, :] = g
        wide_g = g.astype(f32)
        bias_c[...] += wide_g[0:8] + wide_g[8:16] + wide_g[16:24] + wide_g[24:32]

    each(parents, 32, normalize)

    for h in range(2):
        def back(c):
            at = pl.ds(pl.multiple_of(feat + h * half + c, 256), 256)
            scaled = (times_transposed(gcomb[...], cw[at, :]) * inv[...]).astype(bf16)
            out_b[h, :, pl.ds(c, 256)] = dot(spread[...], scaled).astype(bf16)

        each(half, 256, back)
        send_all(out_b, in_b, h, 2 + h)

    stores = []

    def store(src, dst):
        made = pltpu.make_async_copy(src, dst, out_sem.at[len(stores)])
        made.start()
        stores.append(made)

    store(emb, emb_h)
    agg_t[...] = agg[...].T

    def comb_grad(c):
        at = pl.ds(c, 256)
        gc[0:feat, at] = dot(pf_t[...], gcomb[:, at]).astype(bf16)
        gc[feat : feat + hidden, at] = dot(agg_t[...], gcomb[:, at]).astype(bf16)

    each(feat, 256, comb_grad)

    x_first = [[1], [2], [4], [8], [16]]
    y_first = [[1], [4], [2], [8], [16]]
    streams = [
        reduce_stream(net, sems, gc, rc, gc_sum, 512 * i, 512, y_first if i % 2 else x_first) for i in range(gc.shape[0] // 512)
    ]
    biases = [bias_stream(net, sems, bias_c, land_c)]

    def turn(active):
        for stream in list(active):
            if next(stream, "end") == "end":
                active.remove(stream)

    turn(streams)
    turn(biases)

    def parent_back(c):
        pgr[:, pl.ds(c, 256)] = times_transposed(gcomb[...], cw[pl.ds(c, 256), :]).astype(bf16)

    each(feat, 256, parent_back)
    store(pgr, pgr_h)
    for _ in range(5):
        turn(streams)
        turn(biases)

    bias_t[...] = jnp.zeros_like(bias_t)
    for h in range(2):
        all_of(out_b, in_b, h, 2 + h).wait_recv()

        def child_back(c):
            at = pl.ds(pl.multiple_of(h * half + c, 256), 256)
            grown = dot(pick_t[...], in_b[h, :, pl.ds(c, 256)])
            g = (grown * slope[:, at]).astype(bf16)
            gnp[:, at] = g
            bias_t[0:1, at] = jnp.sum(g.astype(f32), axis=0, keepdims=True)
            gt[pl.ds(h * feat, feat), pl.ds(c, 256)] = dot(ci_t[...], g).astype(bf16)

        each(half, 256, child_back)
        more = [
            reduce_stream(net, sems, gt, rt, gt_sum, h * feat + 512 * i, 512, y_first if i % 2 else x_first)
            for i in range(feat // 512)
        ]
        streams += more
        turn(more)

    def into_child(c):
        at = pl.ds(c, 256)
        g_in = times_transposed(gnp[...], nw[at, :])
        is_board = mask[...] > 0.5
        g = jnp.where(is_board, g_in, 0.0).astype(bf16)
        gbd[:, at] = g
        cgr[:, at] = jnp.where(is_board, 0.0, g_in).astype(bf16)
        bias_t[1:2, at] = jnp.sum(g.astype(f32), axis=0, keepdims=True)

    each(feat, 256, into_child)
    for h in range(2):
        def board_grad(c):
            at = pl.ds(pl.multiple_of(h * half + c, 256), 256)
            gt[pl.ds(2 * feat + h * board, board), pl.ds(c, 256)] = dot(cf_t[...], gbd[:, at]).astype(bf16)

        each(half, 256, board_grad)
    more = [
        reduce_stream(net, sems, gt, rt, gt_sum, 2 * feat + board * i, board, y_first if i % 2 else x_first) for i in range(2)
    ]
    streams += more
    turn(more)
    biases.append(bias_stream(net, sems, bias_t, land_t))
    turn(biases)

    def board_back(c):
        at = pl.ds(c, 256)
        left = times_transposed(gbd[...], bp[at, :])
        cgr[:, at] = jnp.where(mask[...] > 0.5, left.astype(bf16), cgr[:, at])

    each(board, 256, board_back)
    store(cgr, cgr_h)
    while streams or biases:
        turn(streams)
        turn(biases)

    store(gc_sum, gc_h)
    for h in range(2):
        store(gt_sum.at[pl.ds(h * feat, feat)], gn_h.at[:, pl.ds(h * half, half)])
        store(gt_sum.at[pl.ds(2 * feat + h * board, board)], gb_h.at[:, pl.ds(h * half, half)])
    store(bias_c, bias_h.at[pl.ds(0, 8)])
    store(bias_t, bias_h.at[pl.ds(8, 8)])
    for which, (out, into) in enumerate([(out_f, in_f), (out_b, in_b)]):
        for h in range(2):
            all_of(out, into, h, 2 * which + h).wait_send()
    for made in stores:
        made.wait()


def fused(n, node, args):
    (child_features, child_type, parent_features, child_slot, parent_slot, importance, board_proj, board_bias,
     neigh_weight, neigh_bias, comb_weight, comb_bias, out_grad) = args
    children, feat = child_features.shape
    parents = parent_features.shape[0]
    board = board_proj.shape[0]
    hidden = neigh_weight.shape[1]
    senders, cap = child_slot.shape[1:]
    edges = senders * cap
    anywhere = pl.BlockSpec(memory_space=pl.ANY)
    vmem = pl.BlockSpec(memory_space=pltpu.VMEM)

    def like(x):
        return pltpu.VMEM(x.shape, x.dtype)

    half = hidden // 2
    steps = n.bit_length() - 1
    grads = pltpu.VMEM((feat + hidden, feat), bf16)
    tail = pltpu.VMEM((2 * feat + 2 * board, half), bf16)
    messages = pltpu.VMEM((2, edges, half), bf16)
    row = pltpu.VMEM((8, feat), f32)
    rows = pltpu.VMEM((steps, 8, feat), f32)
    copies = 10 * steps * 2 + 2 * steps
    out_shape = (
        jax.ShapeDtypeStruct((parents, feat), bf16),
        jax.ShapeDtypeStruct((children, feat), bf16),
        jax.ShapeDtypeStruct((parents, feat), bf16),
        jax.ShapeDtypeStruct((feat + hidden, feat), bf16),
        jax.ShapeDtypeStruct((feat, hidden), bf16),
        jax.ShapeDtypeStruct((board, feat), bf16),
        jax.ShapeDtypeStruct((16, feat), f32),
    )
    result = pl.pallas_call(
        functools.partial(kernel, n, node),
        out_shape=out_shape,
        in_specs=[vmem] * 7 + [anywhere] * 6,
        out_specs=[anywhere] * 7,
        scratch_shapes=[
            like(child_features), like(parent_features), like(board_proj), like(neigh_weight), like(comb_weight), like(out_grad),
            pltpu.VMEM((children, 1), f32),
            pltpu.VMEM((children, feat), bf16),
            pltpu.VMEM((children, hidden), f32),
            pltpu.VMEM((children, hidden), bf16),
            pltpu.VMEM((edges, children), bf16),
            pltpu.VMEM((children, edges), bf16),
            pltpu.VMEM((edges, parents), bf16),
            pltpu.VMEM((parents, edges), bf16),
            pltpu.VMEM((parents, 1), f32),
            messages, messages, messages, messages,
            pltpu.VMEM((parents, feat), f32),
            pltpu.VMEM((parents, hidden), bf16),
            pltpu.VMEM((hidden, parents), bf16),
            pltpu.VMEM((feat, parents), bf16),
            pltpu.VMEM((feat, children), bf16),
            pltpu.VMEM((board, children), bf16),
            pltpu.VMEM((parents, feat), bf16),
            pltpu.VMEM((children, hidden), bf16),
            pltpu.VMEM((parents, feat), bf16),
            grads, grads, grads, tail, tail, tail, row, row, rows, rows,
            pltpu.SemaphoreType.DMA((6,)),
            pltpu.SemaphoreType.DMA((10,)),
            pltpu.SemaphoreType.DMA((4,)),
            pltpu.SemaphoreType.DMA((4,)),
            pltpu.SemaphoreType.DMA((copies,)),
            pltpu.SemaphoreType.DMA((copies,)),
        ],
        compiler_params=pltpu.CompilerParams(
            collective_id=0, has_side_effects=True, vmem_limit_bytes=60 << 20
        ),
    )(
        child_type.reshape(-1, 128), child_slot[0], parent_slot[0], importance[0],
        board_bias[None], neigh_bias[None], comb_bias[None],
        child_features, parent_features, board_proj, neigh_weight, comb_weight, out_grad,
    )
    embedding, child_grad, parent_grad, comb_sum, neigh_sum, board_sum, biases = result
    return (
        embedding, child_grad, parent_grad,
        board_sum.astype(f32), biases[9], neigh_sum.astype(f32), biases[8], comb_sum.astype(f32), jnp.sum(biases[0:8], axis=0),
    )


def send(buffer):
    return lax.all_to_all(buffer, AXES, split_axis=0, concat_axis=0, tiled=True)


def plain(args):
    (child_features, child_type, parent_features, child_slot, parent_slot, importance, board_proj, board_bias,
     neigh_weight, neigh_bias, comb_weight, comb_bias, out_grad) = args
    width_board = board_proj.shape[0]
    child_count, feat_width = child_features.shape
    parent_count = parent_features.shape[0]
    hidden_width = neigh_weight.shape[1]
    senders, capacity = child_slot.shape[1:]
    board = (child_type == 1)[:, None]
    left_part = child_features[:, :width_board]
    board_pre = dot(left_part, board_proj) + board_bias
    child_in = jnp.where(board, board_pre.astype(bf16), child_features)
    neigh_pre = dot(child_in, neigh_weight) + neigh_bias
    neigh = jax.nn.silu(neigh_pre).astype(bf16)
    child_rows = child_slot.reshape(-1)
    outgoing = jnp.take(neigh, child_rows, axis=0).reshape(senders, capacity, hidden_width)
    incoming = send(outgoing).reshape(senders * capacity, hidden_width)
    weights = importance.reshape(-1).astype(f32)
    targets = parent_slot.reshape(-1)
    matches = targets[None, :] == jnp.arange(parent_count, dtype=jnp.int32)[:, None]
    weighted = jnp.where(matches, weights[None, :], 0.0)
    total = jnp.maximum(jnp.sum(weighted, axis=1), 1.0)
    agg = dot(weighted.astype(bf16), incoming) / total[:, None]
    cat = jnp.concatenate([parent_features, agg.astype(bf16)], axis=1)
    comb_pre = dot(cat, comb_weight) + comb_bias
    hidden_z = jax.nn.silu(comb_pre)
    inverse = lax.rsqrt(jnp.sum(hidden_z * hidden_z, axis=1, keepdims=True) + epsilon)
    normed = hidden_z * inverse
    grad_y = out_grad.astype(f32)
    grad_z = inverse * (grad_y - normed * jnp.sum(normed * grad_y, axis=1, keepdims=True))
    grad_comb = (grad_z * silu_slope(comb_pre)).astype(bf16)
    grad_cat = times_transposed(grad_comb, comb_weight)
    grad_scaled = grad_cat[:, feat_width:] / total[:, None]
    grad_edges = (jnp.take(grad_scaled, targets, axis=0) * weights[:, None]).astype(bf16)
    returned = send(grad_edges.reshape(senders, capacity, hidden_width))
    grad_neigh = jax.ops.segment_sum(
        returned.reshape(senders * capacity, hidden_width).astype(f32), child_rows, num_segments=child_count
    )
    grad_npre = (grad_neigh * silu_slope(neigh_pre)).astype(bf16)
    grad_in = times_transposed(grad_npre, neigh_weight)
    grad_board = jnp.where(board, grad_in, 0.0).astype(bf16)
    grad_left = times_transposed(grad_board, board_proj)
    padding = jnp.zeros((child_count, feat_width - width_board), f32)
    child_grad = jnp.where(board, jnp.concatenate([grad_left, padding], axis=1), grad_in).astype(bf16)
    summed = lax.psum(
        (
            outer_sum(left_part, grad_board), jnp.sum(grad_board.astype(f32), axis=0),
            outer_sum(child_in, grad_npre), jnp.sum(grad_npre.astype(f32), axis=0),
            outer_sum(cat, grad_comb), jnp.sum(grad_comb.astype(f32), axis=0),
        ),
        AXES,
    )
    return (normed.astype(bf16), child_grad, grad_cat[:, :feat_width].astype(bf16)) + tuple(summed)


def solution(mesh):
    hop, node = mesh.shape["hop"], mesh.shape["node"]
    n = hop * node

    def body(*args):
        cap = args[3].shape[2]
        if n == 32 and node == 8 and cap % 16 == 0:
            return fused(n, node, args)
        return plain(args)

    rows, cube = P(AXES, None), P(AXES, None, None)
    in_specs = (rows, P(AXES), rows, cube, cube, cube, P(), P(), P(), P(), P(), P(), rows)
    out_specs = (rows, rows, rows, P(), P(), P(), P(), P(), P())
    return jax.shard_map(body, mesh=mesh, in_specs=in_specs, out_specs=out_specs, check_vma=False)
```

```python
import functools

import jax
import jax.numpy as jnp
from jax import lax
from jax.experimental import pallas as pl
from jax.experimental.pallas import tpu as pltpu
from jax.sharding import PartitionSpec as P

epsilon = 1e-06
MESH = pl.DeviceIdType.MESH
AXES = ("hop", "node")
K2_LIMIT = 36
X_FIRST = [[1], [2], [4], [8], [16]]
Y_FIRST = [[1], [4], [2], [8], [16]]
X_DIRECT = [[1], [2], [4], [8, 16]]
Y_DIRECT = [[1], [4], [2], [8, 16]]
COMB_ORDERS = [X_FIRST, Y_FIRST] * 4
TAIL_ORDERS = [X_DIRECT, Y_DIRECT, Y_DIRECT, X_DIRECT, Y_DIRECT, X_DIRECT]
PLAN = (
    "S0", "S1", "G0", "c0", "G1", "c0", "c1", "G2", "c0", "c1", "c2", "G3", "BC", "P", "c0", "c1", "c2", "c3", "bc",
    "A0", "c0", "c1", "c2", "c3", "A1", "BT", "c0", "c1", "c2", "c3", "n0", "n1", "I",
)
LATE = ("c0", "c1", "c2", "c3", "bc", "n0", "n1", "bt")
f32, bf16 = jnp.float32, jnp.bfloat16


def dot(a, b):
    return jnp.dot(a, b, preferred_element_type=f32)


def outer_sum(left, right):
    return lax.dot_general(left, right, (((0,), (0,)), ((), ())), preferred_element_type=f32)


def times_transposed(left, right):
    return lax.dot_general(left, right, (((1,), (1,)), ((), ())), preferred_element_type=f32)


def silu_slope(value):
    sigma = jax.nn.sigmoid(value)
    return sigma * (1.0 + value * (1.0 - sigma))


def each(count, size, step):
    def one(index, carry):
        step(pl.multiple_of(index * size, size))
        return carry

    lax.fori_loop(0, count // size, one, 0)


class Net:
    def __init__(self, n, node):
        self.n, self.node = n, node
        self.me = lax.axis_index("hop") * node + lax.axis_index("node")
        self.bits = [1 << b for b in range(n.bit_length() - 1)]
        self.bit = {b: (self.me // b) % 2 for b in self.bits}

    def partner(self, mask):
        index = 0
        for b in self.bits:
            index = index + ((self.bit[b] + (mask // b) % 2) % 2) * b
        return (index // self.node, index % self.node), index


class Sems:
    def __init__(self, send, recv):
        self.send, self.recv, self.used = send, recv, 0

    def copy(self, src, dst, where):
        at = self.used
        self.used += 1
        made = pltpu.make_async_remote_copy(
            src_ref=src, dst_ref=dst, send_sem=self.send.at[at], recv_sem=self.recv.at[at],
            device_id=where, device_id_type=MESH,
        )
        made.start()
        return made


def reduce_stream(net, sems, grad, landing, full, own_sem, first, rows, stages):
    off, length, land = 0, rows, first
    trail = []
    for bits in stages:
        ways = 1 << len(bits)
        part = length // ways
        mine = sum(net.bit[b] * (1 << i) for i, b in enumerate(bits))
        sent = []
        for c in range(1, ways):
            mask = sum(b for i, b in enumerate(bits) if (c >> i) & 1)
            theirs = sum(((net.bit[b] + ((c >> i) & 1)) % 2) * (1 << i) for i, b in enumerate(bits))
            src = grad.at[pl.ds(pl.multiple_of(first + off + theirs * part, 16), part)]
            dst = landing.at[pl.ds(land + (c - 1) * part, part)]
            sent.append(sems.copy(src, dst, net.partner(mask)[0]))
        yield
        for made in sent:
            made.wait()
        keep = off + mine * part
        block = min(part, 64)

        def add(r):
            at = pl.ds(pl.multiple_of(first + keep + r, 16), block)
            total = grad[at, :].astype(f32)
            for c in range(1, ways):
                total = total + landing[pl.ds(pl.multiple_of(land + (c - 1) * part + r, 16), block), :].astype(f32)
            grad[at, :] = total.astype(bf16)

        each(part, block, add)
        trail.append((bits, off, length))
        off, length, land = keep, part, land + (ways - 1) * part
    source = grad.at[pl.ds(pl.multiple_of(first + off, 16), length)]
    own = pltpu.make_async_copy(source, full.at[pl.ds(pl.multiple_of(off, 16), length)], own_sem)
    own.start()
    for bits, whole, size in reversed(trail):
        at = full.at[pl.ds(pl.multiple_of(off, 16), length)]
        if source is None:
            source = at
        sent = []
        for c in range(1, 1 << len(bits)):
            mask = sum(b for i, b in enumerate(bits) if (c >> i) & 1)
            sent.append(sems.copy(source, at, net.partner(mask)[0]))
        yield
        if own is not None:
            own.wait()
        for made in sent:
            made.wait()
        off, length, source, own = whole, size, None, None


def bias_stream(net, sems, total, landing):
    for i, b in enumerate(net.bits):
        made = sems.copy(total, landing.at[i], net.partner(b)[0])
        yield
        made.wait()
        total[...] = total[...] + landing[i]


def kernel(
    n, node,
    ct_h, cs_h, ps_h, im_h, bb_h, nb_h, cb_h, cf_h, pf_h, bp_h, nw_h, cw_h, og_h,
    emb_h, cgr_h, pgr_h, c0_h, c1_h, c2_h, c3_h, n0_h, n1_h, bias_h,
    ct, cs, ps, im, bb, nb, cb, cf, pf, bp, nw, cw, og,
    mask, ci, slope, ng, pick, pick_t, spread, spread_t, inv,
    out_f, in_f, in_b,
    comb, agg, pf_t, left_t,
    grad, landing, bias_c, bias_t, land_c, land_t,
    in_sem, out_sem, own_sem, a_send, a_recv, r_send, r_recv,
):
    pgr, cgr, gbd, agg_t, gnp, out_b, emb, gcomb = ng, pf, og, pick, spread_t, out_f, cf, ci
    net = Net(n, node)
    sems = Sems(r_send, r_recv)
    me = net.me
    senders, cap = cs.shape
    edges = senders * cap
    children, feat = cf.shape
    parents = pf.shape[0]
    board = bp.shape[0]
    hidden = nw.shape[1]
    half = hidden // 2

    barrier = pltpu.get_barrier_semaphore()

    def greet(i, carry):
        pl.semaphore_signal(barrier, inc=1, device_id=net.partner(i)[0], device_id_type=MESH)
        return carry

    lax.fori_loop(1, n, greet, 0)

    loads = {}
    for i, (name, src, dst) in enumerate(
        [
            ("cs", cs_h, cs), ("ct", ct_h, ct), ("bb", bb_h, bb), ("nb", nb_h, nb), ("cf", cf_h, cf), ("bp", bp_h, bp), ("nw", nw_h, nw),
            ("ps", ps_h, ps), ("im", im_h, im), ("cb", cb_h, cb), ("pf", pf_h, pf), ("cw", cw_h, cw), ("og", og_h, og),
        ]
    ):
        loads[name] = pltpu.make_async_copy(src, dst, in_sem.at[i])
        loads[name].start()

    for name in ("cs", "ct", "bb", "nb"):
        loads[name].wait()
    wide = 128
    eye = lax.broadcasted_iota(jnp.int32, (wide, wide), 0) == lax.broadcasted_iota(jnp.int32, (wide, wide), 1)
    for q in range(ct.shape[0]):
        row = ct[q : q + 1, :].astype(f32)
        mask[pl.ds(q * wide, wide), :] = jnp.sum(jnp.where(eye, row, 0.0), axis=1, keepdims=True)
    small = lax.broadcasted_iota(jnp.int32, (cap, cap), 0) == lax.broadcasted_iota(jnp.int32, (cap, cap), 1)

    def column(ref, s):
        return jnp.sum(jnp.where(small, ref[pl.ds(s, 1), :].astype(f32), 0.0), axis=1, keepdims=True)

    child_lane = lax.broadcasted_iota(jnp.int32, (cap, children), 1).astype(f32)
    parent_lane = lax.broadcasted_iota(jnp.int32, (cap, parents), 1).astype(f32)

    def make_pick(s, carry):
        hit = column(cs, s) == child_lane
        pick[pl.ds(pl.multiple_of(s * cap, 16), cap), :] = jnp.where(hit, 1.0, 0.0).astype(bf16)
        return carry

    lax.fori_loop(0, senders, make_pick, 0)

    loads["cf"].wait()
    loads["bp"].wait()

    def project(c):
        at = pl.ds(c, 256)
        pre = dot(cf[:, 0:board], bp[:, at]) + bb[:, at]
        ci[:, at] = jnp.where(mask[...] > 0.5, pre.astype(bf16), cf[:, at])

    each(feat, 256, project)
    loads["nw"].wait()

    def transform(c):
        at = pl.ds(c, 256)
        pre = dot(ci[...], nw[:, at]) + nb[:, at]
        slope[:, at] = pre
        ng[:, at] = (pre * jax.nn.sigmoid(pre)).astype(bf16)

    each(hidden, 256, transform)

    a_order = n // 2

    def send_all(out, into, h, which):
        def one(i, carry):
            far = i % 2 == 0
            m = jnp.where(far, n - 1 - i // 2, (i + 1) // 2)
            where, index = net.partner(m)
            pltpu.make_async_remote_copy(
                src_ref=out.at[h, pl.ds(pl.multiple_of(index * cap, 16), cap)],
                dst_ref=into.at[h, pl.ds(pl.multiple_of(me * cap, 16), cap)],
                send_sem=a_send.at[which], recv_sem=a_recv.at[which],
                device_id=where, device_id_type=MESH,
            ).start()
            return carry

        lax.fori_loop(0, n - 1, one, 0)
        own = pl.ds(pl.multiple_of(me * cap, 16), cap)
        into[h, own, :] = out[h, own, :]

    def all_of(out, into, h, which):
        return pltpu.make_async_remote_copy(
            src_ref=out.at[h, pl.ds(0, edges - cap)], dst_ref=into.at[h, pl.ds(0, edges - cap)],
            send_sem=a_send.at[which], recv_sem=a_recv.at[which],
            device_id=net.partner(1)[0], device_id_type=MESH,
        )

    for h in range(2):
        def gather(c):
            out_f[h, :, pl.ds(c, 256)] = dot(pick[...], ng[:, pl.ds(pl.multiple_of(h * half + c, 256), 256)]).astype(bf16)

        each(half, 256, gather)
        if h == 0:
            pl.semaphore_wait(barrier, n - 1)
        send_all(out_f, in_f, h, h)

    for name in ("ps", "im", "cb"):
        loads[name].wait()

    def make_spread(s, carry):
        hit = column(ps, s) == parent_lane
        spread[pl.ds(pl.multiple_of(s * cap, 16), cap), :] = jnp.where(hit, column(im, s), 0.0).astype(bf16)
        return carry

    lax.fori_loop(0, senders, make_spread, 0)
    spread_t[...] = spread[...].T
    totals = dot(spread_t[...], jnp.ones((edges, 128), bf16))
    inv[...] = 1.0 / jnp.maximum(totals[:, 0:1], 1.0)
    loads["pf"].wait()
    loads["cw"].wait()
    loads["og"].wait()

    def parent_part(c):
        at = pl.ds(c, 256)
        comb[:, at] = dot(pf[...], cw[0:feat, at]) + cb[:, at]

    each(feat, 256, parent_part)
    pick_t[...] = pick[...].T
    pf_t[...] = pf[...].T
    left_t[0:feat, :] = ci[...].T
    left_t[feat : feat + board, :] = jnp.where(mask[...] > 0.5, cf[:, 0:board], jnp.zeros((), bf16)).T

    def to_slope(r):
        at = pl.ds(r, 32)
        slope[at, :] = silu_slope(slope[at, :])

    each(children, 32, to_slope)

    for h in range(2):
        all_of(out_f, in_f, h, h).wait_recv()

        def aggregate(c):
            sums = dot(spread_t[...], in_f[h, :, pl.ds(c, 256)]) * inv[...]
            agg[:, pl.ds(pl.multiple_of(h * half + c, 256), 256)] = sums.astype(bf16)

        each(half, 256, aggregate)

        def combine(c):
            at = pl.ds(c, 256)
            comb[:, at] += dot(agg[:, h * half : (h + 1) * half], cw[feat + h * half : feat + (h + 1) * half, at])

        each(feat, 256, combine)

    bias_c[...] = jnp.zeros_like(bias_c)

    def normalize(r):
        at = pl.ds(r, 32)
        pre = comb[at, :]
        sigma = jax.nn.sigmoid(pre)
        z = pre * sigma
        inverse = lax.rsqrt(jnp.sum(z * z, axis=1, keepdims=True) + epsilon)
        y = z * inverse
        emb[at, :] = y.astype(bf16)
        gy = og[at, :].astype(f32)
        gz = inverse * (gy - y * jnp.sum(y * gy, axis=1, keepdims=True))
        g = (gz * (sigma * (1.0 + pre * (1.0 - sigma)))).astype(bf16)
        gcomb[at, :] = g
        wide_g = g.astype(f32)
        bias_c[...] += wide_g[0:8] + wide_g[8:16] + wide_g[16:24] + wide_g[24:32]

    each(parents, 32, normalize)

    stores = []

    def store(src, dst):
        made = pltpu.make_async_copy(src, dst, out_sem.at[len(stores)])
        made.start()
        stores.append(made)

    groups = {}
    streams = []

    sums = dict(c0=c0_h, c1=c1_h, c2=c2_h, c3=c3_h, n0=n0_h, n1=n1_h)

    def begin(name, first, orders):
        groups[name] = []
        for i, stages in enumerate(orders):
            to = sums[name].at[pl.ds(512 * i, 512)]
            streams.append(first)
            groups[name].append(reduce_stream(
                net, sems, grad, landing, to, own_sem.at[len(streams) - 1], first + 512 * i, 512, stages
            ))
        turn(name)

    def turn(name):
        for stream in list(groups[name]):
            if next(stream, "end") == "end":
                groups[name].remove(stream)

    def send_back(h):
        def back(c):
            at = pl.ds(pl.multiple_of(feat + h * half + c, 256), 256)
            scaled = (times_transposed(gcomb[...], cw[at, :]) * inv[...]).astype(bf16)
            out_b[h, :, pl.ds(c, 256)] = dot(spread[...], scaled).astype(bf16)

        all_of(out_f, in_f, h, h).wait_send()
        each(half, 256, back)
        send_all(out_b, in_b, h, 2 + h)

    def comb_sum(k):
        h, part = k // 2, k % 2
        if k == 1:
            agg_t[...] = agg[...].T
        left = agg_t if part else pf_t
        base = k * feat

        def comb_grad(c):
            at = pl.ds(pl.multiple_of(h * half + c, 256), 256)
            grad[pl.ds(base, feat), pl.ds(c, 256)] = dot(left[...], gcomb[:, at]).astype(bf16)

        each(half, 256, comb_grad)
        begin("c%d" % k, base, COMB_ORDERS[2 * k : 2 * k + 2])

    def parent_out():
        def parent_back(c):
            pgr[:, pl.ds(c, 256)] = times_transposed(gcomb[...], cw[pl.ds(c, 256), :]).astype(bf16)

        each(feat, 256, parent_back)
        store(emb, emb_h)
        store(pgr, pgr_h)

    def child_sum(h):
        all_of(out_b, in_b, h, 2 + h).wait_recv()
        first = 4 * feat + h * (feat + board)

        def child_back(c):
            at = pl.ds(pl.multiple_of(h * half + c, 256), 256)
            grown = dot(pick_t[...], in_b[h, :, pl.ds(c, 256)])
            g = (grown * slope[:, at]).astype(bf16)
            gnp[:, at] = g
            grad[pl.ds(first, feat + board), pl.ds(c, 256)] = dot(left_t[...], g).astype(bf16)

        each(half, 256, child_back)
        begin("n%d" % h, first, TAIL_ORDERS[3 * h : 3 * h + 3])

    def bias_sum(name, total, landing_rows):
        groups[name] = [bias_stream(net, sems, total, landing_rows)]
        turn(name)

    def child_biases():
        bias_t[...] = jnp.zeros_like(bias_t)

        def sums_of(c):
            at = pl.ds(c, 256)
            g = gnp[:, at].astype(f32)
            bias_t[0:1, at] = jnp.sum(g, axis=0, keepdims=True)
            bias_t[1:2, at] = jnp.sum(jnp.where(mask[...] > 0.5, g, 0.0), axis=0, keepdims=True)

        each(hidden, 256, sums_of)
        bias_sum("bt", bias_t, land_t)

    def child_out():
        def into_child(c):
            at = pl.ds(c, 256)
            g_in = times_transposed(gnp[...], nw[at, :])
            is_board = mask[...] > 0.5
            gbd[:, at] = jnp.where(is_board, g_in, 0.0).astype(bf16)
            cgr[:, at] = jnp.where(is_board, 0.0, g_in).astype(bf16)

        each(feat, 256, into_child)

        def board_back(c):
            at = pl.ds(c, 256)
            left = times_transposed(gbd[...], bp[at, :])
            cgr[:, at] = jnp.where(mask[...] > 0.5, left.astype(bf16), cgr[:, at])

        each(board, 256, board_back)
        store(cgr, cgr_h)

    tasks = {
        "S0": lambda: send_back(0), "S1": lambda: send_back(1),
        "G0": lambda: comb_sum(0), "G1": lambda: comb_sum(1), "G2": lambda: comb_sum(2), "G3": lambda: comb_sum(3),
        "A0": lambda: child_sum(0), "A1": lambda: child_sum(1),
        "BC": lambda: bias_sum("bc", bias_c, land_c), "BT": child_biases, "P": parent_out, "I": child_out,
    }
    for token in PLAN:
        if token in tasks:
            tasks[token]()
        else:
            turn(token)
    while any(groups.values()):
        for name in LATE:
            turn(name)

    bias_h[0:8, :] = bias_c[...]
    bias_h[8:16, :] = bias_t[...]
    for h in range(2):
        all_of(out_b, in_b, h, 2 + h).wait_send()
    for made in stores:
        made.wait()


def widen(
    bias_ref, c0_h, c1_h, c2_h, c3_h, n0_h, n1_h, nw_h, emb_h, cgr_h, pgr_h,
    comb_o, neigh_o, proj_o, emb_o, cgr_o, pgr_o, comb_b, neigh_b, proj_b,
    sums, nw, wide, emb, cgr, pgr, sum_sem, nw_sem, row_sem, out_sem,
):
    feat = nw.shape[0]
    board = proj_o.shape[0]
    half = feat // 2
    block = 512
    per = feat // block

    def piece(i):
        if i < 2 * per:
            at = pl.ds((i % per) * block, block)
            return [(c0_h, c1_h)[i // per].at[at], (c2_h, c3_h)[i // per].at[at]]
        at = pl.ds((i - 2 * per) * block, block)
        return [n0_h.at[at], n1_h.at[at]]

    chunks = [pl.ds(i * block, block) for i in range(sums.shape[1] // block)]
    loads = [
        [pltpu.make_async_copy(src, sums.at[h, at], sum_sem.at[2 * i + h]) for h, src in enumerate(piece(i))]
        for i, at in enumerate(chunks)
    ]
    load_nw = pltpu.make_async_copy(nw_h, nw, nw_sem)
    rows = [(emb_h, emb, emb_o), (cgr_h, cgr, cgr_o), (pgr_h, pgr, pgr_o)]
    row_loads = [pltpu.make_async_copy(src, mid, row_sem.at[i]) for i, (src, mid, _) in enumerate(rows)]
    for made in row_loads + sum(loads, []):
        made.start()
    load_nw.start()
    stores = []

    def store(src, dst):
        made = pltpu.make_async_copy(src, dst, out_sem.at[len(stores)])
        made.start()
        stores.append(made)

    for made, (_, mid, dst) in zip(row_loads, rows):
        made.wait()
        store(mid, dst)
    for i, at in enumerate(chunks):
        for made in loads[i]:
            made.wait()
        if i * block < 3 * feat:
            for h in range(2):
                wide[at, h * half : (h + 1) * half] = sums[h, at, :].astype(f32)
            if i * block < 2 * feat:
                store(wide.at[at], comb_o.at[at])
            else:
                store(wide.at[at], neigh_o.at[pl.ds(i * block - 2 * feat, block)])
    load_nw.wait()
    for r in range(0, board, block):
        at = pl.ds(3 * feat + r, block)
        wide[at, :] = times_transposed(sums[0, at, :], nw[:, 0:half]) + times_transposed(sums[1, at, :], nw[:, half:])
        store(wide.at[at], proj_o.at[pl.ds(r, block)])
    comb_b[...] = jnp.sum(bias_ref[0:8, :], axis=0, keepdims=True)
    neigh_b[...] = bias_ref[8:9, :]
    line = jnp.broadcast_to(bias_ref[9:10, :], (16, feat))
    high = line.astype(bf16)
    rest = line - high.astype(f32)
    low = rest.astype(bf16)
    lowest = (rest - low.astype(f32)).astype(bf16)
    parts = [times_transposed(x, nw[...]) for x in (high, low, lowest)]
    proj_b[...] = (parts[0] + (parts[1] + parts[2]))[0:1]
    for made in stores:
        made.wait()


def fused(n, node, args):
    (child_features, child_type, parent_features, child_slot, parent_slot, importance, board_proj, board_bias,
     neigh_weight, neigh_bias, comb_weight, comb_bias, out_grad) = args
    children, feat = child_features.shape
    parents = parent_features.shape[0]
    board = board_proj.shape[0]
    hidden = neigh_weight.shape[1]
    senders, cap = child_slot.shape[1:]
    edges = senders * cap
    anywhere = pl.BlockSpec(memory_space=pl.ANY)
    vmem = pl.BlockSpec(memory_space=pltpu.VMEM)
    in_hbm = pl.BlockSpec(memory_space=pltpu.HBM)

    def like(x):
        return pltpu.VMEM(x.shape, x.dtype)

    small = (
        child_type.reshape(-1, 128), child_slot[0], parent_slot[0], importance[0],
        board_bias[None], neigh_bias[None], comb_bias[None],
    )
    half = hidden // 2
    steps = n.bit_length() - 1
    grads = pltpu.VMEM((6 * feat + 2 * board, half), bf16)
    messages = pltpu.VMEM((2, edges, half), bf16)
    row = pltpu.VMEM((8, feat), f32)
    rows = pltpu.VMEM((steps, 8, feat), f32)
    copies = 14 * 14 + 2 * steps
    out_shape = (
        jax.ShapeDtypeStruct((parents, feat), bf16),
        jax.ShapeDtypeStruct((children, feat), bf16),
        jax.ShapeDtypeStruct((parents, feat), bf16),
        *[jax.ShapeDtypeStruct((feat, half), bf16)] * 4,
        *[jax.ShapeDtypeStruct((feat + board, half), bf16)] * 2,
        jax.ShapeDtypeStruct((16, feat), f32),
    )
    result = pl.pallas_call(
        functools.partial(kernel, n, node),
        out_shape=out_shape,
        in_specs=[in_hbm] * 13,
        out_specs=[anywhere] * 9 + [vmem],
        scratch_shapes=[
            *[like(x) for x in small],
            like(child_features), like(parent_features), like(board_proj), like(neigh_weight), like(comb_weight), like(out_grad),
            pltpu.VMEM((children, 1), f32),
            pltpu.VMEM((children, feat), bf16),
            pltpu.VMEM((children, hidden), f32),
            pltpu.VMEM((children, hidden), bf16),
            pltpu.VMEM((edges, children), bf16),
            pltpu.VMEM((children, edges), bf16),
            pltpu.VMEM((edges, parents), bf16),
            pltpu.VMEM((parents, edges), bf16),
            pltpu.VMEM((parents, 1), f32),
            messages, messages, messages,
            pltpu.VMEM((parents, feat), f32),
            pltpu.VMEM((parents, hidden), bf16),
            pltpu.VMEM((feat, parents), bf16),
            pltpu.VMEM((feat + board, children), bf16),
            grads, grads, row, row, rows, rows,
            pltpu.SemaphoreType.DMA((13,)),
            pltpu.SemaphoreType.DMA((3,)),
            pltpu.SemaphoreType.DMA((14,)),
            pltpu.SemaphoreType.DMA((4,)),
            pltpu.SemaphoreType.DMA((4,)),
            pltpu.SemaphoreType.DMA((copies,)),
            pltpu.SemaphoreType.DMA((copies,)),
        ],
        compiler_params=pltpu.CompilerParams(
            collective_id=0, has_side_effects=True, vmem_limit_bytes=46 << 20
        ),
    )(
        *[pltpu.with_memory_space_constraint(x, pltpu.HBM) for x in small],
        child_features, parent_features, board_proj, neigh_weight, comb_weight, out_grad,
    )
    embedding, child_grad, parent_grad = result[:3]
    row_out = jax.ShapeDtypeStruct((1, feat), f32)
    total = 3 * feat + board
    chunks = total // 512
    comb_g, neigh_g, proj_g, embedding, child_grad, parent_grad, comb_b, neigh_b, proj_b = pl.pallas_call(
        widen,
        out_shape=(
            jax.ShapeDtypeStruct((2 * feat, feat), f32), jax.ShapeDtypeStruct((feat, hidden), f32),
            jax.ShapeDtypeStruct((board, feat), f32), out_shape[0], out_shape[1], out_shape[2], row_out, row_out, row_out,
        ),
        in_specs=[vmem] + [anywhere] * 4 + [in_hbm] * 2 + [anywhere] * 4,
        out_specs=[anywhere] * 6 + [vmem] * 3,
        scratch_shapes=[
            pltpu.VMEM((2, total, half), bf16), like(neigh_weight), pltpu.VMEM((total, feat), f32),
            like(embedding), like(child_grad), like(parent_grad),
            pltpu.SemaphoreType.DMA((2 * chunks,)), pltpu.SemaphoreType.DMA, pltpu.SemaphoreType.DMA((3,)),
            pltpu.SemaphoreType.DMA((chunks + 3,)),
        ],
        compiler_params=pltpu.CompilerParams(vmem_limit_bytes=K2_LIMIT << 20),
    )(result[9], *result[3:7], *[pltpu.with_memory_space_constraint(x, pltpu.HBM) for x in result[7:9]], neigh_weight, embedding, child_grad, parent_grad)
    return embedding, child_grad, parent_grad, proj_g, proj_b[0], neigh_g, neigh_b[0], comb_g, comb_b[0]


def send(buffer):
    return lax.all_to_all(buffer, AXES, split_axis=0, concat_axis=0, tiled=True)


def plain(args):
    (child_features, child_type, parent_features, child_slot, parent_slot, importance, board_proj, board_bias,
     neigh_weight, neigh_bias, comb_weight, comb_bias, out_grad) = args
    width_board = board_proj.shape[0]
    child_count, feat_width = child_features.shape
    parent_count = parent_features.shape[0]
    hidden_width = neigh_weight.shape[1]
    senders, capacity = child_slot.shape[1:]
    board = (child_type == 1)[:, None]
    left_part = child_features[:, :width_board]
    board_pre = dot(left_part, board_proj) + board_bias
    child_in = jnp.where(board, board_pre.astype(bf16), child_features)
    neigh_pre = dot(child_in, neigh_weight) + neigh_bias
    neigh = jax.nn.silu(neigh_pre).astype(bf16)
    child_rows = child_slot.reshape(-1)
    outgoing = jnp.take(neigh, child_rows, axis=0).reshape(senders, capacity, hidden_width)
    incoming = send(outgoing).reshape(senders * capacity, hidden_width)
    weights = importance.reshape(-1).astype(f32)
    targets = parent_slot.reshape(-1)
    matches = targets[None, :] == jnp.arange(parent_count, dtype=jnp.int32)[:, None]
    weighted = jnp.where(matches, weights[None, :], 0.0)
    total = jnp.maximum(jnp.sum(weighted, axis=1), 1.0)
    agg = dot(weighted.astype(bf16), incoming) / total[:, None]
    cat = jnp.concatenate([parent_features, agg.astype(bf16)], axis=1)
    comb_pre = dot(cat, comb_weight) + comb_bias
    hidden_z = jax.nn.silu(comb_pre)
    inverse = lax.rsqrt(jnp.sum(hidden_z * hidden_z, axis=1, keepdims=True) + epsilon)
    normed = hidden_z * inverse
    grad_y = out_grad.astype(f32)
    grad_z = inverse * (grad_y - normed * jnp.sum(normed * grad_y, axis=1, keepdims=True))
    grad_comb = (grad_z * silu_slope(comb_pre)).astype(bf16)
    grad_cat = times_transposed(grad_comb, comb_weight)
    grad_scaled = grad_cat[:, feat_width:] / total[:, None]
    grad_edges = (jnp.take(grad_scaled, targets, axis=0) * weights[:, None]).astype(bf16)
    returned = send(grad_edges.reshape(senders, capacity, hidden_width))
    grad_neigh = jax.ops.segment_sum(
        returned.reshape(senders * capacity, hidden_width).astype(f32), child_rows, num_segments=child_count
    )
    grad_npre = (grad_neigh * silu_slope(neigh_pre)).astype(bf16)
    grad_in = times_transposed(grad_npre, neigh_weight)
    grad_board = jnp.where(board, grad_in, 0.0).astype(bf16)
    grad_left = times_transposed(grad_board, board_proj)
    padding = jnp.zeros((child_count, feat_width - width_board), f32)
    child_grad = jnp.where(board, jnp.concatenate([grad_left, padding], axis=1), grad_in).astype(bf16)
    summed = lax.psum(
        (
            outer_sum(left_part, grad_board), jnp.sum(grad_board.astype(f32), axis=0),
            outer_sum(child_in, grad_npre), jnp.sum(grad_npre.astype(f32), axis=0),
            outer_sum(cat, grad_comb), jnp.sum(grad_comb.astype(f32), axis=0),
        ),
        AXES,
    )
    return (normed.astype(bf16), child_grad, grad_cat[:, :feat_width].astype(bf16)) + tuple(summed)


def solution(mesh):
    hop, node = mesh.shape["hop"], mesh.shape["node"]
    n = hop * node

    def body(*args):
        cap = args[3].shape[2]
        if n == 32 and node == 8 and cap % 16 == 0:
            return fused(n, node, args)
        return plain(args)

    rows, cube = P(AXES, None), P(AXES, None, None)
    in_specs = (rows, P(AXES), rows, cube, cube, cube, P(), P(), P(), P(), P(), P(), rows)
    out_specs = (rows, rows, rows, P(), P(), P(), P(), P(), P())
    return jax.shard_map(body, mesh=mesh, in_specs=in_specs, out_specs=out_specs, check_vma=False)
```

```python
import functools

import jax
import jax.numpy as jnp
from jax import lax
from jax.experimental import pallas as pl
from jax.experimental.pallas import tpu as pltpu
from jax.sharding import PartitionSpec as P

epsilon = 1e-06
MESH = pl.DeviceIdType.MESH
AXES = ("hop", "node")
K2_LIMIT = 36
WIDTHS = (256, 512, 256)
NORM_UNROLL = 2
COMBINE_UNROLL = 2


def orders(halving, doubling=None):
    return halving, doubling or halving[::-1]


X_FIRST = orders([[1], [2], [4], [8], [16]])
Y_FIRST = orders([[1], [4], [2], [8], [16]])
X_DIRECT = orders([[1], [2], [4], [8, 16]])
Y_DIRECT = orders([[1], [4], [2], [8, 16]])
Z_DIRECT = orders([[1], [8, 16], [4], [2]])
COMB_ORDERS = [X_FIRST, Y_FIRST] * 4
TAIL_ORDERS = [X_DIRECT, Z_DIRECT, Y_DIRECT] * 2 + [X_DIRECT, Y_DIRECT, X_DIRECT]
PLAN = (
    "S0", "S1", "S2", "G0", "c0", "G1", "c0", "c1", "G2", "c0", "c1", "c2", "G3", "BC", "P", "c0", "c1", "c2", "c3", "bc",
    "A0", "c0", "c1", "c2", "c3", "A1", "c0", "n0", "A2", "BT", "c0", "c1", "c2", "c3", "n0", "n1", "n2", "I",
)
LATE = ("c0", "c1", "c2", "c3", "bc", "n0", "n1", "n2", "bt")
f32, bf16 = jnp.float32, jnp.bfloat16


STARTS = tuple(sum(WIDTHS[:h]) for h in range(len(WIDTHS)))


def wide_of(width):
    return 256 if width % 256 == 0 else 128


def dot(a, b):
    return jnp.dot(a, b, preferred_element_type=f32)


def outer_sum(left, right):
    return lax.dot_general(left, right, (((0,), (0,)), ((), ())), preferred_element_type=f32)


def times_transposed(left, right):
    return lax.dot_general(left, right, (((1,), (1,)), ((), ())), preferred_element_type=f32)


def silu_slope(value):
    sigma = jax.nn.sigmoid(value)
    return sigma * (1.0 + value * (1.0 - sigma))


def each(count, size, step, unroll=1):
    def one(index, carry):
        step(pl.multiple_of(index * size, size))
        return carry

    lax.fori_loop(0, count // size, one, 0, unroll=unroll)


class Net:
    def __init__(self, n, node):
        self.n, self.node = n, node
        self.me = lax.axis_index("hop") * node + lax.axis_index("node")
        self.bits = [1 << b for b in range(n.bit_length() - 1)]
        self.bit = {b: (self.me // b) % 2 for b in self.bits}

        low = [b for b in self.bits if b < node]
        self.outer = {m: self.joined(m * node, self.bits[len(low):]) // node for m in range(n // node)}
        self.inner = {m: self.joined(m, low) for m in range(node)}

    def joined(self, mask, bits):
        return sum((1 - self.bit[b] if mask & b else self.bit[b]) * b for b in bits)

    def partner(self, mask):
        if isinstance(mask, int):
            return (self.outer[mask // self.node], self.inner[mask % self.node]), None
        index = 0
        for b in self.bits:
            index = index + ((self.bit[b] + (mask // b) % 2) % 2) * b
        return (index // self.node, index % self.node), index


class Sems:
    def __init__(self, send, recv):
        self.send, self.recv, self.used = send, recv, 0

    def copy(self, src, dst, where):
        at = self.used
        self.used += 1
        made = pltpu.make_async_remote_copy(
            src_ref=src, dst_ref=dst, send_sem=self.send.at[at], recv_sem=self.recv.at[at],
            device_id=where, device_id_type=MESH,
        )
        made.start()
        return made


def reduce_stream(net, sems, grad, landing, full, own_sem, first, rows, order):
    stages, back = order
    off, length, land = 0, rows, first
    sizes = {}
    for bits in stages:
        ways = 1 << len(bits)
        part = length // ways
        mine = sum(net.bit[b] * (1 << i) for i, b in enumerate(bits))
        sizes.update({b: part << i for i, b in enumerate(bits)})
        sent = []
        for c in range(1, ways):
            mask = sum(b for i, b in enumerate(bits) if (c >> i) & 1)
            theirs = sum(((net.bit[b] + ((c >> i) & 1)) % 2) * (1 << i) for i, b in enumerate(bits))
            src = grad.at[pl.ds(pl.multiple_of(first + off + theirs * part, 16), part)]
            dst = landing.at[pl.ds(land + (c - 1) * part, part)]
            sent.append(sems.copy(src, dst, net.partner(mask)[0]))
        yield
        for made in sent:
            made.wait()
        keep = off + mine * part
        block = min(part, 64)

        def add(r):
            at = pl.ds(pl.multiple_of(first + keep + r, 16), block)
            total = grad[at, :].astype(f32)
            for c in range(1, ways):
                total = total + landing[pl.ds(pl.multiple_of(land + (c - 1) * part + r, 16), block), :].astype(f32)
            grad[at, :] = total.astype(bf16)

        each(part, block, add)
        off, length, land = keep, part, land + (ways - 1) * part
    source = grad.at[pl.ds(pl.multiple_of(first + off, 16), length)]
    own = pltpu.make_async_copy(source, full.at[pl.ds(pl.multiple_of(off, 16), length)], own_sem)
    own.start()
    done = []
    for bits in back:
        starts, run, apart = [sum(net.bit[b] * sizes[b] for b in sizes if b not in done)], length, []
        for b in sorted(done, key=sizes.get):
            if sizes[b] == run:
                run *= 2
            else:
                apart.append(b)
        for b in apart:
            starts = starts + [start + sizes[b] for start in starts]
        sent = []
        for c in range(1, 1 << len(bits)):
            mask = sum(b for i, b in enumerate(bits) if (c >> i) & 1)
            for start in starts:
                at = full.at[pl.ds(pl.multiple_of(start, 16), run)]
                sent.append(sems.copy(at if done else source, at, net.partner(mask)[0]))
        yield
        if not done:
            own.wait()
        for made in sent:
            made.wait()
        done = done + bits


def bias_stream(net, sems, total, landing):
    for i, b in enumerate(net.bits):
        made = sems.copy(total, landing.at[i], net.partner(b)[0])
        yield
        made.wait()
        total[...] = total[...] + landing[i]


def kernel(
    n, node,
    ct_h, cs_h, ps_h, im_h, bb_h, nb_h, cb_h, cf_h, pf_h, bp_h, nw_h, cw_h, og_h,
    emb_h, cgr_h, pgr_h, c0_h, c1_h, c2_h, c3_h, n0_h, n1_h, n2_h, bias_h,
    ct, cs, ps, im, bb, nb, cb, cf, pf, bp, nw, cw, og,
    mask, ci, slope, ng, pick, pick_t, spread, spread_t, inv,
    out_0, out_1, out_2, in_f0, in_f1, in_f2, in_b0, in_b1, in_b2,
    comb, agg, pf_t, left_t,
    grad, landing, g_n0, g_n1, g_n2, l_n0, l_n1, l_n2, bias_c, bias_t, land_c, land_t,
    in_sem, out_sem, own_sem, a_send, a_recv, r_send, r_recv,
):
    pgr, cgr, gbd, agg_t, gnp, emb, gcomb = ng, pf, og, pick, spread_t, cf, ci
    out, in_f, in_b = (out_0, out_1, out_2), (in_f0, in_f1, in_f2), (in_b0, in_b1, in_b2)
    net = Net(n, node)
    sems = Sems(r_send, r_recv)
    me = net.me
    senders, cap = cs.shape
    edges = senders * cap
    children, feat = cf.shape
    parents = pf.shape[0]
    board = bp.shape[0]
    hidden = nw.shape[1]
    half = hidden // 2

    barrier = pltpu.get_barrier_semaphore()

    for other in range(n - 1, 0, -1):
        pl.semaphore_signal(barrier, inc=1, device_id=net.partner(other)[0], device_id_type=MESH)

    loads = {}
    for i, (name, src, dst) in enumerate(
        [
            ("cs", cs_h, cs), ("ct", ct_h, ct), ("bb", bb_h, bb), ("nb", nb_h, nb), ("cf", cf_h, cf), ("bp", bp_h, bp), ("nw", nw_h, nw),
            ("ps", ps_h, ps), ("im", im_h, im), ("cb", cb_h, cb), ("pf", pf_h, pf), ("cw", cw_h, cw), ("og", og_h, og),
        ]
    ):
        loads[name] = pltpu.make_async_copy(src, dst, in_sem.at[i])
        loads[name].start()

    for name in ("cs", "ct", "bb", "nb"):
        loads[name].wait()
    wide = 128
    eye = lax.broadcasted_iota(jnp.int32, (wide, wide), 0) == lax.broadcasted_iota(jnp.int32, (wide, wide), 1)
    for q in range(ct.shape[0]):
        row = ct[q : q + 1, :].astype(f32)
        mask[pl.ds(q * wide, wide), :] = jnp.sum(jnp.where(eye, row, 0.0), axis=1, keepdims=True)
    small = lax.broadcasted_iota(jnp.int32, (cap, cap), 0) == lax.broadcasted_iota(jnp.int32, (cap, cap), 1)

    def column(ref, s):
        return jnp.sum(jnp.where(small, ref[pl.ds(s, 1), :].astype(f32), 0.0), axis=1, keepdims=True)

    child_lane = lax.broadcasted_iota(jnp.int32, (cap, children), 1).astype(f32)
    parent_lane = lax.broadcasted_iota(jnp.int32, (cap, parents), 1).astype(f32)

    def make_pick(s, carry):
        hit = column(cs, s) == child_lane
        pick[pl.ds(pl.multiple_of(s * cap, 16), cap), :] = jnp.where(hit, 1.0, 0.0).astype(bf16)
        return carry

    lax.fori_loop(0, senders, make_pick, 0)

    loads["cf"].wait()
    loads["bp"].wait()

    def project(c):
        at = pl.ds(c, 256)
        pre = dot(cf[:, 0:board], bp[:, at]) + bb[:, at]
        ci[:, at] = jnp.where(mask[...] > 0.5, pre.astype(bf16), cf[:, at])

    each(feat, 256, project)
    loads["nw"].wait()

    def transform(c):
        at = pl.ds(c, 256)
        pre = dot(ci[...], nw[:, at]) + nb[:, at]
        slope[:, at] = pre
        ng[:, at] = (pre * jax.nn.sigmoid(pre)).astype(bf16)

    each(hidden, 256, transform)

    a_order = n // 2

    def send_all(into, h, which):
        def one(i, carry):
            far = i % 2 == 0
            m = jnp.where(far, n - 1 - i // 2, (i + 1) // 2)
            where, index = net.partner(m)
            pltpu.make_async_remote_copy(
                src_ref=out[h].at[pl.ds(pl.multiple_of(index * cap, 16), cap)],
                dst_ref=into[h].at[pl.ds(pl.multiple_of(me * cap, 16), cap)],
                send_sem=a_send.at[which], recv_sem=a_recv.at[which],
                device_id=where, device_id_type=MESH,
            ).start()
            return carry

        lax.fori_loop(0, n - 1, one, 0)
        own = pl.ds(pl.multiple_of(me * cap, 16), cap)
        into[h][own, :] = out[h][own, :]

    def all_of(into, h, which):
        return pltpu.make_async_remote_copy(
            src_ref=out[h].at[pl.ds(0, edges - cap)], dst_ref=into[h].at[pl.ds(0, edges - cap)],
            send_sem=a_send.at[which], recv_sem=a_recv.at[which],
            device_id=net.partner(1)[0], device_id_type=MESH,
        )

    for h, (start, width) in enumerate(zip(STARTS, WIDTHS)):
        def gather(c):
            out[h][:, pl.ds(c, step)] = dot(pick[...], ng[:, pl.ds(pl.multiple_of(start + c, step), step)]).astype(bf16)

        step = wide_of(width)
        each(width, step, gather)
        if h == 0:
            pl.semaphore_wait(barrier, n - 1)
        send_all(in_f, h, h)

    for name in ("ps", "im", "cb"):
        loads[name].wait()

    def make_spread(s, carry):
        hit = column(ps, s) == parent_lane
        spread[pl.ds(pl.multiple_of(s * cap, 16), cap), :] = jnp.where(hit, column(im, s), 0.0).astype(bf16)
        return carry

    lax.fori_loop(0, senders, make_spread, 0)
    spread_t[...] = spread[...].T
    totals = dot(spread_t[...], jnp.ones((edges, 128), bf16))
    inv[...] = 1.0 / jnp.maximum(totals[:, 0:1], 1.0)
    loads["pf"].wait()
    loads["cw"].wait()
    loads["og"].wait()

    def parent_part(c):
        at = pl.ds(c, 256)
        comb[:, at] = dot(pf[...], cw[0:feat, at]) + cb[:, at]

    each(feat, 256, parent_part)
    pick_t[...] = pick[...].T
    pf_t[...] = pf[...].T
    left_t[0:feat, :] = ci[...].T
    left_t[feat : feat + board, :] = jnp.where(mask[...] > 0.5, cf[:, 0:board], jnp.zeros((), bf16)).T

    def to_slope(r):
        at = pl.ds(r, 32)
        slope[at, :] = silu_slope(slope[at, :])

    each(children, 32, to_slope)

    for h, (start, width) in enumerate(zip(STARTS, WIDTHS)):
        all_of(in_f, h, h).wait_recv()

        def aggregate(c):
            sums = dot(spread_t[...], in_f[h][:, pl.ds(c, step)]) * inv[...]
            agg[:, pl.ds(pl.multiple_of(start + c, step), step)] = sums.astype(bf16)

        step = wide_of(width)
        each(width, step, aggregate)

        def combine(c):
            at = pl.ds(c, 256)
            comb[:, at] += dot(agg[:, start : start + width], cw[feat + start : feat + start + width, at])

        each(feat, 256, combine, COMBINE_UNROLL)

    bias_c[...] = jnp.zeros_like(bias_c)

    def normalize(r):
        at = pl.ds(r, 32)
        pre = comb[at, :]
        sigma = jax.nn.sigmoid(pre)
        z = pre * sigma
        gy = og[at, :].astype(f32)
        squares = jnp.sum(z * z, axis=1, keepdims=True)
        along = jnp.sum(z * gy, axis=1, keepdims=True)
        inverse = lax.rsqrt(squares + epsilon)
        y = z * inverse
        emb[at, :] = y.astype(bf16)
        gz = inverse * (gy - y * (inverse * along))
        g = (gz * (sigma * (1.0 + pre * (1.0 - sigma)))).astype(bf16)
        gcomb[at, :] = g
        wide_g = g.astype(f32)
        bias_c[...] += wide_g[0:8] + wide_g[8:16] + wide_g[16:24] + wide_g[24:32]

    each(parents, 32, normalize, NORM_UNROLL)

    stores = []

    def store(src, dst):
        made = pltpu.make_async_copy(src, dst, out_sem.at[len(stores)])
        made.start()
        stores.append(made)

    groups = {}
    streams = []

    sums = dict(c0=c0_h, c1=c1_h, c2=c2_h, c3=c3_h, n0=n0_h, n1=n1_h, n2=n2_h)
    child_grads, child_landing = (g_n0, g_n1, g_n2), (l_n0, l_n1, l_n2)

    def begin(name, grad, landing, first, orders):
        groups[name] = []
        for i, stages in enumerate(orders):
            to = sums[name].at[pl.ds(512 * i, 512)]
            streams.append(first)
            groups[name].append(reduce_stream(
                net, sems, grad, landing, to, own_sem.at[len(streams) - 1], first + 512 * i, 512, stages
            ))
        turn(name)

    def turn(name):
        for stream in list(groups[name]):
            if next(stream, "end") == "end":
                groups[name].remove(stream)

    def send_back(h):
        def back(c):
            at = pl.ds(pl.multiple_of(feat + STARTS[h] + c, step), step)
            scaled = (times_transposed(gcomb[...], cw[at, :]) * inv[...]).astype(bf16)
            out[h][:, pl.ds(c, step)] = dot(spread[...], scaled).astype(bf16)

        all_of(in_f, h, h).wait_send()
        step = wide_of(WIDTHS[h])
        each(WIDTHS[h], step, back)
        send_all(in_b, h, 3 + h)

    def comb_sum(k):
        h, part = k // 2, k % 2
        if k == 1:
            agg_t[...] = agg[...].T
        left = agg_t if part else pf_t
        base = k * feat

        def comb_grad(c):
            at = pl.ds(pl.multiple_of(h * half + c, 256), 256)
            grad[pl.ds(base, feat), pl.ds(c, 256)] = dot(left[...], gcomb[:, at]).astype(bf16)

        each(half, 256, comb_grad)
        begin("c%d" % k, grad, landing, base, COMB_ORDERS[2 * k : 2 * k + 2])

    def parent_out():
        def parent_back(c):
            pgr[:, pl.ds(c, 256)] = times_transposed(gcomb[...], cw[pl.ds(c, 256), :]).astype(bf16)

        each(feat, 256, parent_back)
        store(emb, emb_h)
        store(pgr, pgr_h)

    def child_sum(h):
        all_of(in_b, h, 3 + h).wait_recv()

        def child_back(c):
            at = pl.ds(pl.multiple_of(STARTS[h] + c, step), step)
            grown = dot(pick_t[...], in_b[h][:, pl.ds(c, step)])
            g = (grown * slope[:, at]).astype(bf16)
            gnp[:, at] = g
            child_grads[h][:, pl.ds(c, step)] = dot(left_t[...], g).astype(bf16)

        step = wide_of(WIDTHS[h])
        each(WIDTHS[h], step, child_back)
        begin("n%d" % h, child_grads[h], child_landing[h], 0, TAIL_ORDERS[3 * h : 3 * h + 3])

    def bias_sum(name, total, landing_rows):
        groups[name] = [bias_stream(net, sems, total, landing_rows)]
        turn(name)

    def child_biases():
        bias_t[...] = jnp.zeros_like(bias_t)

        def sums_of(c):
            at = pl.ds(c, 256)
            g = gnp[:, at].astype(f32)
            bias_t[0:1, at] = jnp.sum(g, axis=0, keepdims=True)
            bias_t[1:2, at] = jnp.sum(jnp.where(mask[...] > 0.5, g, 0.0), axis=0, keepdims=True)

        each(hidden, 256, sums_of)
        bias_sum("bt", bias_t, land_t)

    def child_out():
        def into_child(c):
            at = pl.ds(c, 256)
            g_in = times_transposed(gnp[...], nw[at, :])
            is_board = mask[...] > 0.5
            gbd[:, at] = jnp.where(is_board, g_in, 0.0).astype(bf16)
            cgr[:, at] = jnp.where(is_board, 0.0, g_in).astype(bf16)

        each(feat, 256, into_child)

        def board_back(c):
            at = pl.ds(c, 256)
            left = times_transposed(gbd[...], bp[at, :])
            cgr[:, at] = jnp.where(mask[...] > 0.5, left.astype(bf16), cgr[:, at])

        each(board, 256, board_back)
        store(cgr, cgr_h)

    tasks = {
        "S0": lambda: send_back(0), "S1": lambda: send_back(1), "S2": lambda: send_back(2),
        "G0": lambda: comb_sum(0), "G1": lambda: comb_sum(1), "G2": lambda: comb_sum(2), "G3": lambda: comb_sum(3),
        "A0": lambda: child_sum(0), "A1": lambda: child_sum(1), "A2": lambda: child_sum(2),
        "BC": lambda: bias_sum("bc", bias_c, land_c), "BT": child_biases, "P": parent_out, "I": child_out,
    }
    for token in PLAN:
        if token in tasks:
            tasks[token]()
        else:
            turn(token)
    while any(groups.values()):
        for name in LATE:
            turn(name)

    bias_h[0:8, :] = bias_c[...]
    bias_h[8:16, :] = bias_t[...]
    for h in range(3):
        all_of(in_b, h, 3 + h).wait_send()
    for made in stores:
        made.wait()


def widen(
    bias_ref, c0_h, c1_h, c2_h, c3_h, n0_h, n1_h, n2_h, nw_h, emb_h, cgr_h, pgr_h,
    comb_o, neigh_o, proj_o, emb_o, cgr_o, pgr_o, comb_b, neigh_b, proj_b,
    sums, nw, wide, emb, cgr, pgr, sum_sem, nw_sem, row_sem, out_sem,
):
    feat = nw.shape[0]
    board = proj_o.shape[0]
    half = feat // 2
    block = 512
    per = feat // block

    def piece(i):
        if i < 2 * per:
            at = pl.ds((i % per) * block, block)
            return [(0, half, (c0_h, c1_h)[i // per].at[at]), (half, half, (c2_h, c3_h)[i // per].at[at])]
        at = pl.ds((i - 2 * per) * block, block)
        return [(start, width, n.at[at]) for start, width, n in zip(STARTS, WIDTHS, (n0_h, n1_h, n2_h))]

    chunks = [pl.ds(i * block, block) for i in range(sums.shape[0] // block)]
    loads = [
        [
            pltpu.make_async_copy(src, sums.at[at, pl.ds(start, width)], sum_sem.at[3 * i + h])
            for h, (start, width, src) in enumerate(piece(i))
        ]
        for i, at in enumerate(chunks)
    ]
    load_nw = pltpu.make_async_copy(nw_h, nw, nw_sem)
    rows = [(emb_h, emb, emb_o), (cgr_h, cgr, cgr_o), (pgr_h, pgr, pgr_o)]
    row_loads = [pltpu.make_async_copy(src, mid, row_sem.at[i]) for i, (src, mid, _) in enumerate(rows)]
    for made in row_loads + sum(loads, []):
        made.start()
    load_nw.start()
    stores = []

    def store(src, dst):
        made = pltpu.make_async_copy(src, dst, out_sem.at[len(stores)])
        made.start()
        stores.append(made)

    for made, (_, mid, dst) in zip(row_loads, rows):
        made.wait()
        store(mid, dst)
    def widened(i):
        at = chunks[i]
        for made in loads[i]:
            made.wait()
        if i * block >= 3 * feat:
            wide[at, :] = times_transposed(sums[at, :], nw[...])
            store(wide.at[at], proj_o.at[pl.ds(i * block - 3 * feat, block)])
            return
        wide[at, :] = sums[at, :].astype(f32)
        if i * block < 2 * feat:
            store(wide.at[at], comb_o.at[at])
        else:
            store(wide.at[at], neigh_o.at[pl.ds(i * block - 2 * feat, block)])

    before = len(chunks) // 2
    for i in range(before):
        widened(i)
    load_nw.wait()
    for i in range(3 * feat // block, len(chunks)):
        widened(i)
    for i in range(before, 3 * feat // block):
        widened(i)
    comb_b[...] = jnp.sum(bias_ref[0:8, :], axis=0, keepdims=True)
    neigh_b[...] = bias_ref[8:9, :]
    line = bias_ref[9:10, :]
    high = line.astype(bf16)
    rest = line - high.astype(f32)
    low = rest.astype(bf16)
    lowest = (rest - low.astype(f32)).astype(bf16)
    parts = jnp.concatenate([jnp.broadcast_to(x.astype(f32), (8, feat)) for x in (high, low, lowest, lowest)], axis=0)
    spun = times_transposed(parts.astype(bf16), nw[...])
    proj_b[...] = spun[0:1] + (spun[8:9] + spun[16:17])
    for made in stores:
        made.wait()


def fused(n, node, args):
    (child_features, child_type, parent_features, child_slot, parent_slot, importance, board_proj, board_bias,
     neigh_weight, neigh_bias, comb_weight, comb_bias, out_grad) = args
    children, feat = child_features.shape
    parents = parent_features.shape[0]
    board = board_proj.shape[0]
    hidden = neigh_weight.shape[1]
    senders, cap = child_slot.shape[1:]
    edges = senders * cap
    anywhere = pl.BlockSpec(memory_space=pl.ANY)
    vmem = pl.BlockSpec(memory_space=pltpu.VMEM)
    in_hbm = pl.BlockSpec(memory_space=pltpu.HBM)

    def like(x):
        return pltpu.VMEM(x.shape, x.dtype)

    small = (
        child_type.reshape(-1, 128), child_slot[0], parent_slot[0], importance[0],
        board_bias[None], neigh_bias[None], comb_bias[None],
    )
    half = hidden // 2
    steps = n.bit_length() - 1
    grads = pltpu.VMEM((4 * feat, half), bf16)
    child_grads = [pltpu.VMEM((feat + board, width), bf16) for width in WIDTHS]
    messages = [pltpu.VMEM((edges, width), bf16) for width in WIDTHS]
    row = pltpu.VMEM((8, feat), f32)
    rows = pltpu.VMEM((steps, 8, feat), f32)
    copies = 17 * 20 + 2 * steps
    out_shape = (
        jax.ShapeDtypeStruct((parents, feat), bf16),
        jax.ShapeDtypeStruct((children, feat), bf16),
        jax.ShapeDtypeStruct((parents, feat), bf16),
        *[jax.ShapeDtypeStruct((feat, half), bf16)] * 4,
        *[jax.ShapeDtypeStruct((feat + board, width), bf16) for width in WIDTHS],
        jax.ShapeDtypeStruct((16, feat), f32),
    )
    result = pl.pallas_call(
        functools.partial(kernel, n, node),
        out_shape=out_shape,
        in_specs=[in_hbm] * 13,
        out_specs=[anywhere] * 10 + [vmem],
        scratch_shapes=[
            *[like(x) for x in small],
            like(child_features), like(parent_features), like(board_proj), like(neigh_weight), like(comb_weight), like(out_grad),
            pltpu.VMEM((children, 1), f32),
            pltpu.VMEM((children, feat), bf16),
            pltpu.VMEM((children, hidden), f32),
            pltpu.VMEM((children, hidden), bf16),
            pltpu.VMEM((edges, children), bf16),
            pltpu.VMEM((children, edges), bf16),
            pltpu.VMEM((edges, parents), bf16),
            pltpu.VMEM((parents, edges), bf16),
            pltpu.VMEM((parents, 1), f32),
            *messages, *messages, *messages,
            pltpu.VMEM((parents, feat), f32),
            pltpu.VMEM((parents, hidden), bf16),
            pltpu.VMEM((feat, parents), bf16),
            pltpu.VMEM((feat + board, children), bf16),
            grads, grads, *child_grads, *child_grads, row, row, rows, rows,
            pltpu.SemaphoreType.DMA((13,)),
            pltpu.SemaphoreType.DMA((3,)),
            pltpu.SemaphoreType.DMA((17,)),
            pltpu.SemaphoreType.DMA((6,)),
            pltpu.SemaphoreType.DMA((6,)),
            pltpu.SemaphoreType.DMA((copies,)),
            pltpu.SemaphoreType.DMA((copies,)),
        ],
        compiler_params=pltpu.CompilerParams(
            collective_id=0, has_side_effects=True, vmem_limit_bytes=46 << 20
        ),
    )(
        *[pltpu.with_memory_space_constraint(x, pltpu.HBM) for x in small],
        child_features, parent_features, board_proj, neigh_weight, comb_weight, out_grad,
    )
    embedding, child_grad, parent_grad = result[:3]
    hold = functools.partial(pltpu.with_memory_space_constraint, memory_space=pltpu.HBM)
    row_out = jax.ShapeDtypeStruct((1, feat), f32)
    total = 3 * feat + board
    chunks = total // 512
    comb_g, neigh_g, proj_g, embedding, child_grad, parent_grad, comb_b, neigh_b, proj_b = pl.pallas_call(
        widen,
        out_shape=(
            jax.ShapeDtypeStruct((2 * feat, feat), f32), jax.ShapeDtypeStruct((feat, hidden), f32),
            jax.ShapeDtypeStruct((board, feat), f32), out_shape[0], out_shape[1], out_shape[2], row_out, row_out, row_out,
        ),
        in_specs=[vmem] + [anywhere] * 11,
        out_specs=[anywhere] * 6 + [vmem] * 3,
        scratch_shapes=[
            pltpu.VMEM((total, feat), bf16), like(neigh_weight), pltpu.VMEM((total, feat), f32),
            like(embedding), like(child_grad), like(parent_grad),
            pltpu.SemaphoreType.DMA((3 * chunks,)), pltpu.SemaphoreType.DMA, pltpu.SemaphoreType.DMA((3,)),
            pltpu.SemaphoreType.DMA((chunks + 3,)),
        ],
        compiler_params=pltpu.CompilerParams(vmem_limit_bytes=K2_LIMIT << 20),
    )(result[10], *result[3:6], hold(result[6]), result[7], hold(result[8]), result[9], neigh_weight, embedding, child_grad, parent_grad)
    return embedding, child_grad, parent_grad, proj_g, proj_b[0], neigh_g, neigh_b[0], comb_g, comb_b[0]


def send(buffer):
    return lax.all_to_all(buffer, AXES, split_axis=0, concat_axis=0, tiled=True)


def plain(args):
    (child_features, child_type, parent_features, child_slot, parent_slot, importance, board_proj, board_bias,
     neigh_weight, neigh_bias, comb_weight, comb_bias, out_grad) = args
    width_board = board_proj.shape[0]
    child_count, feat_width = child_features.shape
    parent_count = parent_features.shape[0]
    hidden_width = neigh_weight.shape[1]
    senders, capacity = child_slot.shape[1:]
    board = (child_type == 1)[:, None]
    left_part = child_features[:, :width_board]
    board_pre = dot(left_part, board_proj) + board_bias
    child_in = jnp.where(board, board_pre.astype(bf16), child_features)
    neigh_pre = dot(child_in, neigh_weight) + neigh_bias
    neigh = jax.nn.silu(neigh_pre).astype(bf16)
    child_rows = child_slot.reshape(-1)
    outgoing = jnp.take(neigh, child_rows, axis=0).reshape(senders, capacity, hidden_width)
    incoming = send(outgoing).reshape(senders * capacity, hidden_width)
    weights = importance.reshape(-1).astype(f32)
    targets = parent_slot.reshape(-1)
    matches = targets[None, :] == jnp.arange(parent_count, dtype=jnp.int32)[:, None]
    weighted = jnp.where(matches, weights[None, :], 0.0)
    total = jnp.maximum(jnp.sum(weighted, axis=1), 1.0)
    agg = dot(weighted.astype(bf16), incoming) / total[:, None]
    cat = jnp.concatenate([parent_features, agg.astype(bf16)], axis=1)
    comb_pre = dot(cat, comb_weight) + comb_bias
    hidden_z = jax.nn.silu(comb_pre)
    inverse = lax.rsqrt(jnp.sum(hidden_z * hidden_z, axis=1, keepdims=True) + epsilon)
    normed = hidden_z * inverse
    grad_y = out_grad.astype(f32)
    grad_z = inverse * (grad_y - normed * jnp.sum(normed * grad_y, axis=1, keepdims=True))
    grad_comb = (grad_z * silu_slope(comb_pre)).astype(bf16)
    grad_cat = times_transposed(grad_comb, comb_weight)
    grad_scaled = grad_cat[:, feat_width:] / total[:, None]
    grad_edges = (jnp.take(grad_scaled, targets, axis=0) * weights[:, None]).astype(bf16)
    returned = send(grad_edges.reshape(senders, capacity, hidden_width))
    grad_neigh = jax.ops.segment_sum(
        returned.reshape(senders * capacity, hidden_width).astype(f32), child_rows, num_segments=child_count
    )
    grad_npre = (grad_neigh * silu_slope(neigh_pre)).astype(bf16)
    grad_in = times_transposed(grad_npre, neigh_weight)
    grad_board = jnp.where(board, grad_in, 0.0).astype(bf16)
    grad_left = times_transposed(grad_board, board_proj)
    padding = jnp.zeros((child_count, feat_width - width_board), f32)
    child_grad = jnp.where(board, jnp.concatenate([grad_left, padding], axis=1), grad_in).astype(bf16)
    summed = lax.psum(
        (
            outer_sum(left_part, grad_board), jnp.sum(grad_board.astype(f32), axis=0),
            outer_sum(child_in, grad_npre), jnp.sum(grad_npre.astype(f32), axis=0),
            outer_sum(cat, grad_comb), jnp.sum(grad_comb.astype(f32), axis=0),
        ),
        AXES,
    )
    return (normed.astype(bf16), child_grad, grad_cat[:, :feat_width].astype(bf16)) + tuple(summed)


def solution(mesh):
    hop, node = mesh.shape["hop"], mesh.shape["node"]
    n = hop * node

    def body(*args):
        cap = args[3].shape[2]
        if n == 32 and node == 8 and cap % 16 == 0:
            return fused(n, node, args)
        return plain(args)

    rows, cube = P(AXES, None), P(AXES, None, None)
    in_specs = (rows, P(AXES), rows, cube, cube, cube, P(), P(), P(), P(), P(), P(), rows)
    out_specs = (rows, rows, rows, P(), P(), P(), P(), P(), P())
    return jax.shard_map(body, mesh=mesh, in_specs=in_specs, out_specs=out_specs, check_vma=False)
```
